256 devices in a mesh: chain: 8 (over x, core), depth: 32 (over y, z).
Axes of the slice: x: 4, y: 4, z: 8, core: 2. Of those that a mesh axis runs over, the one named last changes fastest.
Arguments:
- model_field: float32 [2048, 2048], P(('chain', 'depth')), parts along dimension 0, may hold values from -4 to 4
- column_rate: float32 [16384], P('chain'), parts along dimension 0, may hold values from 0.2 to 20
- wavelets: float32 [128, 2048], P('chain'), parts along dimension 0, may hold values from -6 to 6
- source_depth: int32 [128], P('chain'), parts along dimension 0, may hold values from 0 to 255
- observed: float32 [2048, 16, 2048], P(('chain', 'depth')), parts along dimension 0, may hold values from -3 to 3
- basis: bfloat16 [2048, 256, 2048], P('chain', 'depth'), parts along dimension 0, may hold values from -0.03125 to 0.03125
- curvature: float32 [2048], P('chain'), parts along dimension 0, may hold values from 0.5 to 50
- noise_draw: float32 [2048, 2048], P(('chain', 'depth')), parts along dimension 0, may hold values from -6 to 6
Outputs:
- proposal: float32 [2048, 2048], P(('chain', 'depth')), parts along dimension 0
- log_gain: float32 [8], P('chain'), parts along dimension 0
The draws below stay inside these ranges and needn't reach their ends.
There are 8 independent parts, one for each index of `chain`. The reference program is written for one: setup_inputs(seed, part) draws one part's arguments, and reference() takes and returns one part's arrays. A program takes and returns all parts, laid end to end along the dimension named above; each array names one. Nothing has to cross between parts.
All inputs are finite; a program needn't handle non-finite values.
Results may differ from the reference program's by a relative error of at most 0.0003.
The reference program's roundings to bfloat16 on the way count: a program that leaves them out, or rounds other values in their place, can miss the bound.
Values sent between devices are 32-bit elements; how exact they have to be, the bound alone decides.
A program may use at most 64 MiB of HBM per device.

```python
import math
import jax
import jax.numpy as jnp
from jax import lax

LAT = 2048
NSRC = 16
RANK = 256
NZ = 256


def with_ends(array, stream_key, low, largest):
    place = [jax.random.randint(jax.random.fold_in(stream_key, axis), (), 0, length) for axis, length in enumerate(array.shape)]
    longest = array.shape.index(max(array.shape))
    neighbour = place[:longest] + [(place[longest] + 1) % array.shape[longest]] + place[longest + 1:]
    return array.at[tuple(place)].set(low).at[tuple(neighbour)].set(largest)


def block_levels(own_key, shape, cuts, least, largest):
    factor_of, own = 1.0, jax.random.fold_in(own_key, 6)
    for dim, parts in cuts:
        heights = jnp.exp(jax.random.uniform(jax.random.fold_in(own, dim), (parts,), jnp.float32, least / len(cuts), largest / len(cuts)))
        factor_of = factor_of * jnp.repeat(heights, shape[dim] // parts).reshape([-1 if axis == dim else 1 for axis in range(len(shape))])
    return factor_of


def noise(own_key, dims, spread, limit, shards=(), kind=jnp.bfloat16):
    gain = block_levels(own_key, dims, shards, -0.22, 0.18) if shards else 1.0
    drawn = jax.random.normal(own_key, dims, jnp.float32) * spread * gain
    return jnp.minimum(jnp.maximum(drawn, -limit), limit).astype(kind)


def setup_inputs(seed: int = 0, part: int = 0) -> dict:
    arg_keys = jax.random.split(jax.random.key(seed), 9)
    own_keys = jax.random.split(jax.random.fold_in(arg_keys[8], part), 9)
    return {
        "model_field": noise(own_keys[0], (NZ, LAT), 1.0, 4.0, ((0, 32),), jnp.float32),
        "column_rate": jnp.clip(jnp.exp(jax.random.uniform(own_keys[1], (LAT,), jnp.float32, math.log(0.2), math.log(20.0))), 0.2, 20.0),
        "wavelets": noise(own_keys[2], (NSRC, LAT), 1.0, 6.0, (), jnp.float32),
        "source_depth": with_ends(jax.random.randint(own_keys[3], (NSRC,), 0, NZ), jax.random.fold_in(own_keys[3], 1), 0, NZ - 1).astype(jnp.int32),
        "observed": noise(own_keys[4], (NZ, NSRC, LAT), 0.5, 3.0, ((0, 32),), jnp.float32),
        "basis": noise(own_keys[5], (RANK, NZ, LAT), (NZ * LAT // 16) ** -0.5, 0.03125, ((1, 32),)),
        "curvature": jnp.clip(jnp.exp(jax.random.uniform(own_keys[6], (RANK,), jnp.float32, math.log(0.5), math.log(50.0))), 0.5, 50.0),
        "noise_draw": noise(own_keys[7], (NZ, LAT), 1.0, 6.0, ((0, 32),), jnp.float32),
    }


def coefficients(model, column_rate, depth_count):
    coef = (column_rate / depth_count)[None, :] * jnp.exp(0.5 * model)
    return (coef, jnp.exp(-coef))

def march_down(decay, wavelets, source_depth):
    layers = jnp.arange(decay.shape[0], dtype=jnp.int32)

    def advance(state, inputs):
        factor, layer = inputs
        inject = jnp.where((source_depth == layer)[:, None], wavelets, jnp.zeros_like(wavelets))
        state = factor[None, :] * state + inject
        return (state, state)
    start = jnp.zeros(wavelets.shape, wavelets.dtype)
    _, fields = lax.scan(advance, start, (decay, layers))
    return fields

def march_up(decay, misfit_field):

    def retreat(carry, inputs):
        factor, resid = inputs
        adjoint = resid + carry
        return (factor[None, :] * adjoint, adjoint)
    start = jnp.zeros(misfit_field.shape[1:], misfit_field.dtype)
    _, adjoints = lax.scan(retreat, start, (decay, misfit_field), reverse=True)
    return adjoints

def energy(model, column_rate, wavelets, source_depth, observed):
    coef, decay = coefficients(model, column_rate, model.shape[0])
    fields = march_down(decay, wavelets, source_depth)
    resid = fields - observed
    value = jnp.sum(resid * resid) / wavelets.shape[0] + 0.5 * jnp.sum(model * model)
    return (value, coef, decay, fields, resid)

def reference(model_field, column_rate, wavelets, source_depth, observed, basis, curvature, noise_draw):
    sources = wavelets.shape[0]
    before, coef, decay, fields, resid = energy(model_field, column_rate, wavelets, source_depth, observed)
    adjoints = march_up(decay, resid)
    previous = jnp.concatenate([jnp.zeros_like(fields[:1]), fields[:-1]], axis=0)
    gradient = model_field - coef * decay / sources * lax.optimization_barrier(jnp.sum(adjoints * previous, axis=1))
    flat_basis = basis.reshape(basis.shape[0], -1)
    stacked = jnp.stack([gradient.reshape(-1), noise_draw.reshape(-1)]).astype(jnp.bfloat16)
    projected = lax.dot_general(stacked, flat_basis, (((1,), (1,)), ((), ())), preferred_element_type=jnp.float32)
    damping = curvature / (1.0 + curvature)
    shrink = 1.0 - 1.0 / jnp.sqrt(1.0 + curvature)
    mixed = (damping * projected[0] - shrink * projected[1]).astype(jnp.bfloat16)
    correction = jnp.dot(mixed, flat_basis, preferred_element_type=jnp.float32).reshape(model_field.shape)
    proposal = model_field - gradient + noise_draw + correction
    after = energy(proposal, column_rate, wavelets, source_depth, observed)[0]
    cells = model_field.shape[0] * model_field.shape[1]
    log_gain = jnp.reshape((before - after) / cells, (1,))
    return (proposal, log_gain)
```

```python
import jax
import jax.numpy as jnp
from jax import lax
from jax.sharding import Mesh
from jax.sharding import PartitionSpec as P

DEPTH = ("depth",)
LANES = 128


def decays(model, column_rate, depth_count):
    coef = (column_rate / depth_count)[None, :] * jnp.exp(0.5 * model)
    return coef, jnp.exp(-coef)


def slab_march(decay, wavelets, source_depth, first, observed):
    layers, sources = decay.shape[0], wavelets.shape[0]
    product, state = None, jnp.zeros_like(wavelets)
    products, own, taps, squares = [], [], jnp.zeros_like(wavelets), 0.0
    for z in range(layers):
        product = decay[z] if z == 0 else product * decay[z]
        state = decay[z][None] * state + jnp.where((source_depth == first + z)[:, None], wavelets, 0.0)
        products.append(product)
        own.append(state)
        taps = taps + product[None] * observed[z]
        squares = squares + product * product
    return products, own, taps, squares


def to_owners(rows, total, squares):
    blocks = rows.shape[1] // LANES
    q = rows.reshape(2, 8, blocks, LANES).transpose(2, 0, 1, 3).reshape(2 * blocks, 8, LANES)
    shared = jnp.stack([total, squares]).reshape(2, blocks, LANES).transpose(1, 0, 2)
    shared = jnp.repeat(shared, 2, axis=0)
    return jnp.concatenate([q, shared], axis=1)


def exchange(blocks):
    return lax.all_to_all(blocks, DEPTH, 0, 0, tiled=True)


def owner_carries(got, sd_half, layers):
    slabs = got.shape[0]
    carries = []
    carry = jnp.zeros_like(got[0, :8])
    for j in range(slabs):
        carries.append(carry)
        inside = jnp.logical_and(sd_half >= j * layers, sd_half < (j + 1) * layers)[:, None]
        carry = got[j, 8:9] * carry + jnp.where(inside, got[j, :8], 0.0)
    return carries


def local(model, column_rate, wavelets, source_depth, observed, basis, curvature, noise):
    layers, width = model.shape
    slabs = lax.axis_size(DEPTH)
    me = lax.axis_index(DEPTH)
    sources = wavelets.shape[0]
    first = me * layers
    above = (source_depth < first)[:, None]
    blocks = width // LANES
    half = me % 2
    sd_half = lax.dynamic_slice_in_dim(source_depth, half * 8, 8)

    coef, decay = decays(model, column_rate, slabs * layers)
    products, own, taps, squares = slab_march(decay, wavelets, source_depth, first, observed)
    got = exchange(to_owners(jnp.where(above, taps, own[-1]), products[-1], squares))
    carries = owner_carries(got, sd_half, layers)
    below = jnp.zeros_like(carries[0])
    back = [None] * slabs
    for i in reversed(range(slabs)):
        over = (sd_half < i * layers)[:, None]
        inside = jnp.logical_and(sd_half >= i * layers, sd_half < (i + 1) * layers)[:, None]
        sent = jnp.where(over, carries[i], jnp.where(inside, below, 0.0))
        rest = jnp.sum(jnp.where(over, below, 0.0), axis=0, keepdims=True)
        back[i] = jnp.concatenate([sent, rest], axis=0)
        below = below + carries[i] * (carries[i] * got[i, 9:10] - got[i, :8])
    mine = exchange(jnp.stack(back))
    sent = mine[:, :8].reshape(blocks, 2, 8, LANES).transpose(1, 2, 0, 3).reshape(sources, width)
    rest = mine[:, 8].reshape(blocks, 2, LANES).sum(1).reshape(width)
    carry = jnp.where(above, sent, 0.0)
    acc = jnp.where(above, 0.0, sent)
    rows, misfit = [None] * layers, 0.0
    for z in reversed(range(layers)):
        field = carry * products[z][None] + own[z]
        resid = field - observed[z]
        misfit = misfit + resid * resid
        acc = acc + field * resid
        rows[z] = rest + jnp.sum(jnp.where((source_depth < first + z)[:, None], acc, 0.0), axis=0)
    gradient = model - coef / sources * jnp.stack(rows)
    gain = jnp.sum(misfit) / sources + 0.5 * jnp.sum(model * model)

    f32 = jnp.float32
    p = jnp.sum(basis.astype(f32) * lax.reduce_precision(gradient, 8, 7)[None], axis=(1, 2))
    q = jnp.sum(basis.astype(f32) * lax.reduce_precision(noise, 8, 7)[None], axis=(1, 2))
    damping = curvature / (1.0 + curvature)
    shrink = 1.0 - 1.0 / jnp.sqrt(1.0 + curvature)
    part = damping * p - shrink * q
    mix = lax.reduce_precision(lax.all_gather(part, DEPTH).sum(0), 8, 7)
    correction = jnp.sum(mix[:, None, None] * basis.astype(f32), axis=0)
    proposal = model - gradient + noise + correction

    _, decay = decays(proposal, column_rate, slabs * layers)
    products, own, taps, squares = slab_march(decay, wavelets, source_depth, first, observed)
    got = exchange(to_owners(jnp.where(above, taps, own[-1]), products[-1], squares))
    misfit = 0.0
    for z in range(layers):
        resid = own[z] - observed[z]
        misfit = misfit + jnp.sum(resid * resid)
    carries = owner_carries(got, sd_half, layers)
    for j in range(slabs):
        misfit = misfit + jnp.sum(carries[j] * (carries[j] * got[j, 9:10] - 2.0 * got[j, :8]))
    gain = gain - (misfit / sources + 0.5 * jnp.sum(proposal * proposal))
    total = lax.all_gather(gain, DEPTH).sum(0)
    return proposal, jnp.reshape(total / (slabs * layers * width), (1,))


def solution(mesh):
    both = ("chain", "depth")
    in_specs = (
        P(both, None), P("chain"), P("chain", None), P("chain"), P(both, None, None),
        P("chain", "depth", None), P("chain"), P(both, None),
    )
    out_specs = (P(both, None), P("chain"))
    return jax.shard_map(local, mesh=mesh, in_specs=in_specs, out_specs=out_specs, check_vma=False)
```

```python
import functools

import jax
import jax.numpy as jnp
from jax import lax
from jax.experimental import pallas as pl
from jax.experimental.pallas import tpu as pltpu
from jax.sharding import PartitionSpec as P

LANES = 128
HALF = 8
F32 = jnp.float32


def columns(c):
    return pl.ds(pl.multiple_of(c * LANES, LANES), LANES)


def kernel(
    slabs, side, layers, sources, width, rank,
    sd_ref, model_hbm, rate_hbm, wave_hbm, obs_hbm, basis_hbm, curv_hbm, noise_hbm,
    prop_ref, gain_ref,
    model, rate, wave, obs, basis, curv, noise,
    sdv, coef, prods, own, wide, grad, rest, pbuf, mixcol, carries,
    out1, out1s, in1, in1s, out2, out2s, in2, in2s,
    out3, in3, out4, out4s, in4, in4s, out5, in5,
    load_sem, send_sem, recv_sem,
):
    me = lax.axis_index("depth")
    blocks = width // LANES
    first = me * layers
    rows = side
    cols = slabs // side
    pieces = 4
    per = rank // pieces

    loads = [
        pltpu.make_async_copy(src, dst, load_sem.at[i])
        for i, (src, dst) in enumerate(
            [(model_hbm, model), (rate_hbm, rate), (wave_hbm, wave), (obs_hbm, obs), (noise_hbm, noise), (curv_hbm, curv)]
        )
    ]
    basis_loads = [
        pltpu.make_async_copy(
            basis_hbm.at[pl.ds(i * per, per)], basis.at[pl.ds(i * per, per)], load_sem.at[len(loads) + i]
        )
        for i in range(pieces)
    ]
    for copy in loads + basis_loads:
        copy.start()

    def spread(size):
        steps = [size // 2]
        for n in range(1, size):
            steps.append((size // 2 - (n + 1) // 2) if n % 2 else (size // 2 + n // 2))
        return steps

    ys = [lax.rem(me // rows + dy, cols) * rows for dy in spread(cols)]
    zs = [lax.rem(lax.rem(me, rows) + dz, rows) for dz in spread(rows)]
    peers = [y + z for z in zs for y in ys][:-1]

    barrier = pltpu.get_barrier_semaphore()
    for other in peers:
        pl.semaphore_signal(barrier, inc=1, device_id={"depth": other}, device_id_type=pl.DeviceIdType.MESH)

    def send(step, other, pairs):
        for n, (block, landing) in enumerate(pairs):
            pltpu.make_async_remote_copy(
                src_ref=block(other),
                dst_ref=landing.at[me],
                send_sem=send_sem.at[step, n],
                recv_sem=recv_sem.at[step, n],
                device_id={"depth": other},
                device_id_type=pl.DeviceIdType.MESH,
            ).start()

    def send_all(step, pairs):
        for other in peers:
            send(step, other, pairs)

    def wait_all(sem, step, landings):
        for n, landing in enumerate(landings):
            part = landing.at[pl.ds(0, slabs - 1)]
            pltpu.make_async_copy(part, part, sem.at[step, n]).wait()

    for copy in loads[:4]:
        copy.wait()

    which = lax.broadcasted_iota(jnp.int32, (sources, LANES), 0)
    where_to = jnp.zeros((sources, LANES), jnp.int32)
    for k in range(sources):
        where_to = jnp.where(which == k, sd_ref[k], where_to)
    sdv[...] = where_to

    def march(c, field, main, shared, keep):
        at = columns(c)
        sd = sdv[...]
        above = sd < first
        factor = (rate[:, at] * (1.0 / (slabs * layers))) * jnp.exp(0.5 * field)
        decay = jnp.exp(-factor)
        if keep:
            coef[:, at] = factor
        source = wave[:, at]
        state = jnp.zeros((sources, LANES), F32)
        taps = jnp.zeros((sources, LANES), F32)
        misfit = jnp.zeros((sources, LANES), F32)
        product = squares = None
        for z in range(layers):
            d = decay[z : z + 1]
            product = d if z == 0 else product * d
            state = d * state + jnp.where(sd == first + z, source, 0.0)
            seen = obs[z, :, at]
            taps = taps + product * seen
            squares = product * product if z == 0 else squares + product * product
            if keep:
                prods[z : z + 1, at] = product
                own[z, :, at] = state
            else:
                miss = state - seen
                misfit = misfit + miss * miss
        block = jnp.where(above, taps, state)
        for h in range(sources // HALF):
            main[2 * c + h] = block[h * HALF : (h + 1) * HALF]
            shared[2 * c + h, 0:1] = product
            shared[2 * c + h, 1:2] = squares
        return misfit[:HALF] + misfit[HALF:]

    @pl.loop(0, blocks)
    def _(c):
        march(c, model[:, columns(c)], out1, out1s, True)

    in1[me] = out1[me]
    in1s[me] = out1s[me]
    pl.semaphore_wait(barrier, slabs - 1)
    send_all(0, [(lambda d: out1.at[d], in1), (lambda d: out1s.at[d], in1s)])

    for copy in loads[4:]:
        copy.wait()

    def project(values, first_time):
        parts = [values[:, c * LANES : (c + 1) * LANES] for c in range(blocks)]
        unroll = 8

        def some(i, _):
            for u in range(unroll):
                r = i * unroll + u
                vector = basis[r].astype(F32) if first_time else wide[r]
                if first_time:
                    wide[r] = vector
                total = vector[:, :LANES] * parts[0]
                for c in range(1, blocks):
                    total = total + vector[:, c * LANES : (c + 1) * LANES] * parts[c]
                pbuf[pl.ds(pl.multiple_of(r * layers, layers), layers), :] = total
            return 0

        for i in range(pieces if first_time else 1):
            if first_time:
                basis_loads[i].wait()
                lax.fori_loop(i * per // unroll, (i + 1) * per // unroll, some, 0)
            else:
                lax.fori_loop(0, rank // unroll, some, 0)
        folded = pbuf[pl.ds(0, rank, stride=layers), :]
        for s in range(1, layers):
            folded = folded + pbuf[pl.ds(s, rank, stride=layers), :]
        return lax.dot_general(
            jnp.ones((8, LANES), F32), folded, (((1,), (1,)), ((), ())),
            precision=lax.Precision.HIGHEST, preferred_element_type=F32,
        )[0:1]

    q = project(noise[...].astype(jnp.bfloat16).astype(F32), True)
    curvature = curv[...]
    damping = curvature / (1.0 + curvature)
    shrink = 1.0 - 1.0 / jnp.sqrt(1.0 + curvature)
    known = shrink * q

    sd_half = sdv[pl.ds(pl.multiple_of(lax.rem(me, 2) * HALF, HALF), HALF), :]
    group = 4

    def inside(j):
        return jnp.logical_and(sd_half >= j * layers, sd_half < (j + 1) * layers)

    wait_all(recv_sem, 0, [in1, in1s])

    def forward(i, carry):
        for u in range(group):
            j = i * group + u
            carries[j] = carry
            carry = in1s[j, 0:1] * carry + jnp.where(inside(j), in1[j], 0.0)
        return carry

    lax.fori_loop(0, slabs // group, forward, jnp.zeros((HALF, LANES), F32))

    def backward(i, below):
        for u in range(group):
            j = slabs - 1 - (i * group + u)
            over = sd_half < j * layers
            carry = carries[j]
            out2[j] = jnp.where(over, carry, jnp.where(inside(j), below, 0.0))
            out2s[j] = jnp.sum(jnp.where(over, below, 0.0), axis=0, keepdims=True)
            below = below + carry * (carry * in1s[j, 1:2] - in1[j])
        return below

    lax.fori_loop(0, slabs // group, backward, jnp.zeros((HALF, LANES), F32))
    in2[me] = out2[me]
    in2s[me] = out2s[me]
    send_all(1, [(lambda d: out2.at[d], in2), (lambda d: out2s.at[d], in2s)])
    wait_all(recv_sem, 1, [in2, in2s])

    layer_of = lax.broadcasted_iota(jnp.int32, (layers, LANES), 0)

    def slab(c, energy):
        at = columns(c)
        sd = sdv[...]
        above = sd < first
        sent = jnp.concatenate([in2[2 * c], in2[2 * c + 1]], axis=0)
        beyond = in2s[2 * c] + in2s[2 * c + 1]
        carry = jnp.where(above, sent, 0.0)
        acc = jnp.where(above, 0.0, sent)
        misfit = jnp.zeros((sources, LANES), F32)
        sums = jnp.zeros((layers, LANES), F32)
        for z in reversed(range(layers)):
            field = carry * prods[z : z + 1, at] + own[z, :, at]
            miss = field - obs[z, :, at]
            misfit = misfit + miss * miss
            acc = acc + field * miss
            held = jnp.where(sd < first + z, acc, 0.0)
            sums = jnp.where(
                layer_of == z, jnp.sum(held[:HALF] + held[HALF:], axis=0, keepdims=True), sums
            )
        old = model[:, at]
        g = old - coef[:, at] * (1.0 / sources) * (beyond + sums)
        grad[:, at] = g.astype(jnp.bfloat16).astype(F32)
        rest[:, at] = old - g + noise[:, at]
        return energy + (misfit[:HALF] + misfit[HALF:]) * (1.0 / sources) + 0.5 * (old * old)

    energy = lax.fori_loop(0, blocks, slab, jnp.zeros((HALF, LANES), F32))

    out3[...] = damping * project(grad[...], False) - known
    in3[me] = out3[...]
    send_all(2, [(lambda d: out3, in3)])
    wait_all(recv_sem, 2, [in3])
    total = in3[0]
    for j in range(1, slabs):
        total = total + in3[j]
    mix = total.astype(jnp.bfloat16).astype(F32)
    for h in range(rank // LANES):
        mixcol[h * LANES : (h + 1) * LANES] = jnp.broadcast_to(
            mix[:, h * LANES : (h + 1) * LANES], (LANES, LANES)
        ).T

    def correct(i, totals):
        unroll = 8
        for u in range(unroll):
            r = i * unroll + u
            weight = jnp.broadcast_to(mixcol[pl.ds(r, 1), :], (layers, LANES))
            vector = wide[r]
            totals = tuple(
                t + vector[:, c * LANES : (c + 1) * LANES] * weight for c, t in enumerate(totals)
            )
        return totals

    start = tuple(rest[:, c * LANES : (c + 1) * LANES] * 0.0 for c in range(blocks))
    correction = lax.fori_loop(0, rank // 8, correct, start)
    for c in range(blocks):
        at = slice(c * LANES, (c + 1) * LANES)
        prop_ref[:, at] = rest[:, at] + correction[c]

    energy_blocks = [(lambda d: out4.at[d], in4), (lambda d: out4s.at[d], in4s)]
    twos = [2 * lax.rem(lax.rem(me, rows) // 2 + dz, rows // 2) for dz in spread(rows // 2)]
    owners = [y + z for z in twos for y in ys]
    for n, owner in enumerate(owners):
        c = owner // 2
        new = prop_ref[:, columns(c)]
        energy = energy - march(c, new, out4, out4s, False) * (1.0 / sources) - 0.5 * (new * new)
        if n > 0:
            send(3, owners[n - 1], energy_blocks)
            send(3, owners[n - 1] + 1, energy_blocks)
    in4[me] = out4[me]
    in4s[me] = out4s[me]
    send(3, 2 * (me // 2) + 1 - lax.rem(me, 2), energy_blocks)
    wait_all(recv_sem, 3, [in4, in4s])

    def last(i, state):
        carry, energy = state
        for u in range(group):
            j = i * group + u
            block = in4[j]
            energy = energy - carry * (carry * in4s[j, 1:2] - 2.0 * block) * (1.0 / sources)
            carry = in4s[j, 0:1] * carry + jnp.where(inside(j), block, 0.0)
        return carry, energy

    _, energy = lax.fori_loop(0, slabs // group, last, (jnp.zeros((HALF, LANES), F32), energy))
    out5[...] = jnp.sum(energy, axis=0, keepdims=True)
    in5[me] = out5[...]
    send_all(4, [(lambda d: out5, in5)])
    wait_all(recv_sem, 4, [in5])
    total = in5[0]
    for j in range(1, slabs):
        total = total + in5[j]
    gain_ref[0] = jnp.sum(total) * (1.0 / (slabs * layers * width))
    for step, landings in enumerate([(in1, in1s), (in2, in2s), (in3,), (in4, in4s), (in5,)]):
        wait_all(send_sem, step, landings)


def hand_over(prop_ref, gain_ref, prop_out, gain_out):
    prop_out[...] = prop_ref[...]
    gain_out[0] = gain_ref[0]


def local(slabs, side, model, column_rate, wavelets, source_depth, observed, basis, curvature, noise):
    layers, width = model.shape
    sources, rank = wavelets.shape[0], basis.shape[0]
    anywhere = pl.BlockSpec(memory_space=pl.ANY)
    vmem = lambda *shape: pltpu.VMEM(shape, F32)
    exchange = lambda: [vmem(slabs, HALF, LANES), vmem(slabs, 2, LANES)] * 2
    prop, gain = pl.pallas_call(
        functools.partial(kernel, slabs, side, layers, sources, width, rank),
        out_shape=(
            jax.ShapeDtypeStruct((layers, width), F32),
            jax.ShapeDtypeStruct((1,), F32),
        ),
        in_specs=[pl.BlockSpec(memory_space=pltpu.SMEM)] + [anywhere] * 7,
        out_specs=(pl.BlockSpec(memory_space=pltpu.VMEM), pl.BlockSpec(memory_space=pltpu.SMEM)),
        scratch_shapes=[
            vmem(layers, width), vmem(1, width), vmem(sources, width), vmem(layers, sources, width),
            pltpu.VMEM((rank, layers, width), jnp.bfloat16), vmem(1, rank), vmem(layers, width),
            pltpu.VMEM((sources, LANES), jnp.int32), vmem(layers, width), vmem(layers, width),
            vmem(layers, sources, width), vmem(rank, layers, width), vmem(layers, width), vmem(layers, width),
            vmem(rank * layers, LANES), vmem(rank, LANES), vmem(slabs, HALF, LANES),
        ]
        + exchange()
        + [vmem(slabs, HALF, LANES), vmem(slabs, 1, LANES)] * 2
        + [vmem(1, rank), vmem(slabs, 1, rank)]
        + exchange()
        + [vmem(1, LANES), vmem(slabs, 1, LANES)]
        + [
            pltpu.SemaphoreType.DMA((10,)),
            pltpu.SemaphoreType.DMA((5, 2)),
            pltpu.SemaphoreType.DMA((5, 2)),
        ],
        compiler_params=pltpu.CompilerParams(
            collective_id=0, has_side_effects=True, vmem_limit_bytes=60 << 20
        ),
    )(
        source_depth, model, column_rate.reshape(1, width), wavelets, observed, basis,
        curvature.reshape(1, rank), noise,
    )
    whole = [pl.BlockSpec(memory_space=pltpu.VMEM), pl.BlockSpec(memory_space=pltpu.SMEM)]
    return pl.pallas_call(
        hand_over,
        out_shape=(jax.ShapeDtypeStruct((layers, width), F32), jax.ShapeDtypeStruct((1,), F32)),
        in_specs=whole,
        out_specs=tuple(whole),
    )(prop, gain)


def solution(mesh):
    both = ("chain", "depth")
    in_specs = (
        P(both, None), P("chain"), P("chain", None), P("chain"), P(both, None, None),
        P("chain", "depth", None), P("chain"), P(both, None),
    )
    out_specs = (P(both, None), P("chain"))
    body = functools.partial(local, mesh.shape["depth"], 8)
    return jax.shard_map(body, mesh=mesh, in_specs=in_specs, out_specs=out_specs, check_vma=False)
```

```python
import functools

import jax
import jax.numpy as jnp
from jax import lax
from jax.experimental import pallas as pl
from jax.experimental.pallas import tpu as pltpu
from jax.sharding import PartitionSpec as P

LANES = 128
HALF = 8
F32 = jnp.float32


def columns(c):
    return pl.ds(pl.multiple_of(c * LANES, LANES), LANES)


def kernel(
    slabs, side, layers, sources, width, rank,
    sd_hbm, model_hbm, rate_hbm, wave_hbm, obs_hbm, basis_hbm, curv_hbm, noise_hbm,
    prop_ref, gain_ref,
    model, rate, wave, obs, basis, curv, noise, sd_ref,
    sdv, coef, prods, own, wide, grad, rest, pbuf, mixcol, carries,
    out1, in1, out2, in2, out3, in3, out4, in4, out5, in5,
    load_sem, send_sem, recv_sem,
):
    me = lax.axis_index("depth")
    blocks = width // LANES
    first = me * layers
    rows = side
    cols = slabs // side
    pieces = 4
    per = rank // pieces

    loads = [
        pltpu.make_async_copy(src, dst, load_sem.at[i])
        for i, (src, dst) in enumerate(
            [(model_hbm, model), (rate_hbm, rate), (wave_hbm, wave), (obs_hbm, obs), (noise_hbm, noise), (curv_hbm, curv), (sd_hbm, sd_ref)]
        )
    ]
    basis_loads = [
        pltpu.make_async_copy(
            basis_hbm.at[pl.ds(i * per, per)], basis.at[pl.ds(i * per, per)], load_sem.at[len(loads) + i]
        )
        for i in range(pieces)
    ]

    def spread(size):
        steps = [size // 2]
        for n in range(1, size):
            steps.append((size // 2 - (n + 1) // 2) if n % 2 else (size // 2 + n // 2))
        return steps

    ys = [lax.rem(me // rows + dy, cols) * rows for dy in spread(cols)]
    zs = [lax.rem(lax.rem(me, rows) + dz, rows) for dz in spread(rows)]
    peers = [y + z for z in zs for y in ys][:-1]

    barrier = pltpu.get_barrier_semaphore()
    for other in peers:
        pl.semaphore_signal(barrier, inc=1, device_id={"depth": other}, device_id_type=pl.DeviceIdType.MESH)

    for copy in loads + basis_loads:
        copy.start()

    def send(step, other, pairs):
        for n, (block, landing) in enumerate(pairs):
            pltpu.make_async_remote_copy(
                src_ref=block(other),
                dst_ref=landing.at[me],
                send_sem=send_sem.at[step, n],
                recv_sem=recv_sem.at[step, n],
                device_id={"depth": other},
                device_id_type=pl.DeviceIdType.MESH,
            ).start()

    def send_all(step, pairs):
        for other in peers:
            send(step, other, pairs)

    def wait_all(sem, step, landings):
        for n, landing in enumerate(landings):
            part = landing.at[pl.ds(0, slabs - 1)]
            pltpu.make_async_copy(part, part, sem.at[step, n]).wait()

    for copy in loads[:4] + loads[6:]:
        copy.wait()

    which = lax.broadcasted_iota(jnp.int32, (sources, LANES), 0)
    where_to = jnp.zeros((sources, LANES), jnp.int32)
    for k in range(sources):
        where_to = jnp.where(which == k, sd_ref[k], where_to)
    sdv[...] = where_to

    def march(c, field, main, keep):
        at = columns(c)
        sd = sdv[...]
        above = sd < first
        factor = (rate[:, at] * (1.0 / (slabs * layers))) * jnp.exp(0.5 * field)
        decay = jnp.exp(-factor)
        if keep:
            coef[:, at] = factor
        source = wave[:, at]
        state = jnp.zeros((sources, LANES), F32)
        taps = jnp.zeros((sources, LANES), F32)
        misfit = jnp.zeros((sources, LANES), F32)
        product = squares = None
        for z in range(layers):
            d = decay[z : z + 1]
            product = d if z == 0 else product * d
            state = d * state + jnp.where(sd == first + z, source, 0.0)
            seen = obs[z, :, at]
            taps = taps + product * seen
            squares = product * product if z == 0 else squares + product * product
            if keep:
                prods[z : z + 1, at] = product
                own[z, :, at] = state
            else:
                miss = state - seen
                misfit = misfit + miss * miss
        block = jnp.where(above, taps, state)
        for h in range(sources // HALF):
            main[2 * c + h, 0:HALF] = block[h * HALF : (h + 1) * HALF]
            main[2 * c + h, HALF : HALF + 1] = product
            main[2 * c + h, HALF + 1 : HALF + 2] = squares
        return misfit[:HALF] + misfit[HALF:]

    @pl.loop(0, blocks)
    def _(c):
        march(c, model[:, columns(c)], out1, True)

    in1[me] = out1[me]
    pl.semaphore_wait(barrier, slabs - 1)
    send_all(0, [(lambda d: out1.at[d], in1)])

    for copy in loads[4:6]:
        copy.wait()

    def project(values, first_time):
        parts = [values[:, c * LANES : (c + 1) * LANES] for c in range(blocks)]
        unroll = 8

        def some(i, _):
            for u in range(unroll):
                r = i * unroll + u
                vector = basis[r].astype(F32) if first_time else wide[r]
                if first_time:
                    wide[r] = vector
                total = vector[:, :LANES] * parts[0]
                for c in range(1, blocks):
                    total = total + vector[:, c * LANES : (c + 1) * LANES] * parts[c]
                pbuf[pl.ds(pl.multiple_of(r * layers, layers), layers), :] = total
            return 0

        for i in range(pieces if first_time else 1):
            if first_time:
                basis_loads[i].wait()
                lax.fori_loop(i * per // unroll, (i + 1) * per // unroll, some, 0)
            else:
                lax.fori_loop(0, rank // unroll, some, 0)
        folded = pbuf[pl.ds(0, rank, stride=layers), :]
        for s in range(1, layers):
            folded = folded + pbuf[pl.ds(s, rank, stride=layers), :]
        high = folded.astype(jnp.bfloat16)
        left = folded - high.astype(F32)
        middle = left.astype(jnp.bfloat16)
        low = (left - middle.astype(F32)).astype(jnp.bfloat16)
        return lax.dot_general(
            jnp.ones((8, 3 * LANES), jnp.bfloat16), jnp.concatenate([high, middle, low], axis=1),
            (((1,), (1,)), ((), ())), preferred_element_type=F32,
        )[0:1]

    q = project(noise[...].astype(jnp.bfloat16).astype(F32), True)
    curvature = curv[...]
    damping = curvature / (1.0 + curvature)
    shrink = 1.0 - 1.0 / jnp.sqrt(1.0 + curvature)
    known = shrink * q

    sd_half = sdv[pl.ds(pl.multiple_of(lax.rem(me, 2) * HALF, HALF), HALF), :]
    group = 4

    def inside(j):
        return jnp.logical_and(sd_half >= j * layers, sd_half < (j + 1) * layers)

    wait_all(recv_sem, 0, [in1])

    def forward(i, carry):
        for u in range(group):
            j = i * group + u
            carries[j] = carry
            carry = in1[j, HALF : HALF + 1] * carry + jnp.where(inside(j), in1[j, 0:HALF], 0.0)
        return carry

    lax.fori_loop(0, slabs // group, forward, jnp.zeros((HALF, LANES), F32))

    def backward(i, below):
        for u in range(group):
            j = slabs - 1 - (i * group + u)
            over = sd_half < j * layers
            carry = carries[j]
            out2[j, 0:HALF] = jnp.where(over, carry, jnp.where(inside(j), below, 0.0))
            out2[j, HALF : HALF + 1] = jnp.sum(jnp.where(over, below, 0.0), axis=0, keepdims=True)
            below = below + carry * (carry * in1[j, HALF + 1 : HALF + 2] - in1[j, 0:HALF])
        return below

    lax.fori_loop(0, slabs // group, backward, jnp.zeros((HALF, LANES), F32))
    in2[me] = out2[me]
    send_all(1, [(lambda d: out2.at[d], in2)])
    wait_all(recv_sem, 1, [in2])

    layer_of = lax.broadcasted_iota(jnp.int32, (layers, LANES), 0)

    def slab(c, energy):
        at = columns(c)
        sd = sdv[...]
        above = sd < first
        sent = jnp.concatenate([in2[2 * c, 0:HALF], in2[2 * c + 1, 0:HALF]], axis=0)
        beyond = in2[2 * c, HALF : HALF + 1] + in2[2 * c + 1, HALF : HALF + 1]
        carry = jnp.where(above, sent, 0.0)
        acc = jnp.where(above, 0.0, sent)
        misfit = jnp.zeros((sources, LANES), F32)
        sums = jnp.zeros((layers, LANES), F32)
        for z in reversed(range(layers)):
            field = carry * prods[z : z + 1, at] + own[z, :, at]
            miss = field - obs[z, :, at]
            misfit = misfit + miss * miss
            acc = acc + field * miss
            held = jnp.where(sd < first + z, acc, 0.0)
            sums = jnp.where(
                layer_of == z, jnp.sum(held[:HALF] + held[HALF:], axis=0, keepdims=True), sums
            )
        old = model[:, at]
        g = old - coef[:, at] * (1.0 / sources) * (beyond + sums)
        grad[:, at] = g.astype(jnp.bfloat16).astype(F32)
        rest[:, at] = old - g + noise[:, at]
        return energy + (misfit[:HALF] + misfit[HALF:]) * (1.0 / sources) + 0.5 * (old * old)

    energy = lax.fori_loop(0, blocks, slab, jnp.zeros((HALF, LANES), F32))

    out3[...] = damping * project(grad[...], False) - known
    in3[me] = out3[...]
    send_all(2, [(lambda d: out3, in3)])
    wait_all(recv_sem, 2, [in3])
    total = in3[0]
    for j in range(1, slabs):
        total = total + in3[j]
    mix = total.astype(jnp.bfloat16).astype(F32)
    for h in range(rank // LANES):
        mixcol[h * LANES : (h + 1) * LANES] = jnp.broadcast_to(
            mix[:, h * LANES : (h + 1) * LANES], (LANES, LANES)
        ).T

    def correct(i, totals):
        unroll = 8
        for u in range(unroll):
            r = i * unroll + u
            weight = jnp.broadcast_to(mixcol[pl.ds(r, 1), :], (layers, LANES))
            vector = wide[r]
            totals = tuple(
                t + vector[:, c * LANES : (c + 1) * LANES] * weight for c, t in enumerate(totals)
            )
        return totals

    start = tuple(rest[:, c * LANES : (c + 1) * LANES] * 0.0 for c in range(blocks))
    correction = lax.fori_loop(0, rank // 8, correct, start)
    for c in range(blocks):
        at = slice(c * LANES, (c + 1) * LANES)
        prop_ref[:, at] = rest[:, at] + correction[c]

    energy_blocks = [(lambda d: out4.at[d], in4)]
    twos = [2 * lax.rem(lax.rem(me, rows) // 2 + dz, rows // 2) for dz in spread(rows // 2)]
    owners = [y + z for z in twos for y in ys]
    for n, owner in enumerate(owners):
        c = owner // 2
        new = prop_ref[:, columns(c)]
        energy = energy - march(c, new, out4, False) * (1.0 / sources) - 0.5 * (new * new)
        if n > 0:
            send(3, owners[n - 1], energy_blocks)
            send(3, owners[n - 1] + 1, energy_blocks)
    in4[me] = out4[me]
    send(3, 2 * (me // 2) + 1 - lax.rem(me, 2), energy_blocks)
    wait_all(recv_sem, 3, [in4])

    def last(i, state):
        carry, energy = state
        for u in range(group):
            j = i * group + u
            block = in4[j, 0:HALF]
            energy = energy - carry * (carry * in4[j, HALF + 1 : HALF + 2] - 2.0 * block) * (1.0 / sources)
            carry = in4[j, HALF : HALF + 1] * carry + jnp.where(inside(j), block, 0.0)
        return carry, energy

    _, energy = lax.fori_loop(0, slabs // group, last, (jnp.zeros((HALF, LANES), F32), energy))
    out5[...] = jnp.sum(energy, axis=0, keepdims=True)
    in5[me] = out5[...]
    send_all(4, [(lambda d: out5, in5)])
    wait_all(recv_sem, 4, [in5])
    total = in5[0]
    for j in range(1, slabs):
        total = total + in5[j]
    gain_ref[...] = total * (1.0 / (slabs * layers * width))
    for step, landings in enumerate([(in1,), (in2,), (in3,), (in4,), (in5,)]):
        wait_all(send_sem, step, landings)


def local(slabs, side, model, column_rate, wavelets, source_depth, observed, basis, curvature, noise):
    layers, width = model.shape
    sources, rank = wavelets.shape[0], basis.shape[0]
    anywhere = pl.BlockSpec(memory_space=pl.ANY)
    vmem = lambda *shape: pltpu.VMEM(shape, F32)
    exchange = lambda rows: [vmem(slabs, HALF + rows, LANES)] * 2
    prop, gain = pl.pallas_call(
        functools.partial(kernel, slabs, side, layers, sources, width, rank),
        out_shape=(pltpu.VMEM((layers, width), F32), pltpu.VMEM((1, LANES), F32)),
        in_specs=[anywhere] * 8,
        out_specs=(pl.BlockSpec(memory_space=pltpu.VMEM), pl.BlockSpec(memory_space=pltpu.VMEM)),
        scratch_shapes=[
            vmem(layers, width), vmem(1, width), vmem(sources, width), vmem(layers, sources, width),
            pltpu.VMEM((rank, layers, width), jnp.bfloat16), vmem(1, rank), vmem(layers, width),
            pltpu.SMEM((sources,), jnp.int32), pltpu.VMEM((sources, LANES), jnp.int32), vmem(layers, width), vmem(layers, width),
            vmem(layers, sources, width), vmem(rank, layers, width), vmem(layers, width), vmem(layers, width),
            vmem(rank * layers, LANES), vmem(rank, LANES), vmem(slabs, HALF, LANES),
        ]
        + exchange(2)
        + exchange(1)
        + [vmem(1, rank), vmem(slabs, 1, rank)]
        + exchange(2)
        + [vmem(1, LANES), vmem(slabs, 1, LANES)]
        + [
            pltpu.SemaphoreType.DMA((12,)),
            pltpu.SemaphoreType.DMA((5, 2)),
            pltpu.SemaphoreType.DMA((5, 2)),
        ],
        compiler_params=pltpu.CompilerParams(
            collective_id=0, has_side_effects=True, vmem_limit_bytes=60 << 20
        ),
    )(
        source_depth, model, column_rate.reshape(1, width), wavelets, observed, basis,
        curvature.reshape(1, rank), noise,
    )
    return prop, jnp.sum(gain, axis=1)


def solution(mesh):
    both = ("chain", "depth")
    in_specs = (
        P(both, None), P("chain"), P("chain", None), P("chain"), P(both, None, None),
        P("chain", "depth", None), P("chain"), P(both, None),
    )
    out_specs = (P(both, None), P("chain"))
    body = functools.partial(local, mesh.shape["depth"], 8)
    return jax.shard_map(body, mesh=mesh, in_specs=in_specs, out_specs=out_specs, check_vma=False)
```
